32 devices in a mesh: occ: 4 (over y, x), vir: 8 (over z, core).
Axes of the slice: x: 2, y: 2, z: 4, core: 2. Of those that a mesh axis runs over, the one named last changes fastest.
Arguments:
- amplitudes: bfloat16 [2048, 16384], P('occ', 'vir'), may hold values from -6 to 6
- integrals: bfloat16 [16384, 512], P('vir', 'occ'), may hold values from -0.09375 to 0.09375
- active: int32 [16, 128], P('occ', 'vir'), may hold values from 0 to 1
Outputs:
- residual: bfloat16 [2048, 512], P('occ', 'vir')
The draws below stay inside these ranges and needn't reach their ends.
All inputs are finite; a program needn't handle non-finite values.
Results may differ from the reference program's by a relative error of at most 0.001.
Values may be sent and summed in bfloat16 or wider, within the bound.
A program may use at most 64 MiB of HBM per device.

```python
import jax
import jax.numpy as jnp
from jax import lax

TILE = 128
OCC_TILES = 16
EF_COUNT = 128
OCC_ROWS = 2048
EF_PAIRS = 16384
AB_PAIRS = 512


def draw_active(key, part):
    tile_index = jnp.arange(OCC_TILES, dtype=jnp.int32)[:, None]
    level = 1 + 6 * tile_index // max(OCC_TILES - 1, 1)
    draws = jax.random.randint(key, (OCC_TILES, EF_COUNT), 0, 8)
    return (draws < level).astype(jnp.int32)


def spiked(values, own_key, source, target, parts, factor):
    def block_of(dim):
        return (jnp.arange(values.shape[dim]) // (values.shape[dim] // parts)).reshape((-1,) + (1,) * (values.ndim - 1 - dim))

    one_side = jax.random.permutation(own_key, parts)[block_of(target)]
    other_side = (block_of(target) + parts // 2) % parts
    return jnp.where((block_of(source) == one_side) | (block_of(source) == other_side), factor * values, values)


def shard_levels(key, shape, pieces, smallest, top_value):
    def one(axis_at, shards_of):
        steps = jax.random.uniform(jax.random.fold_in(jax.random.fold_in(key, 6), axis_at), (shards_of,), jnp.float32, smallest / len(pieces), top_value / len(pieces))
        return jnp.repeat(jnp.exp(steps), shape[axis_at] // shards_of).reshape((-1,) + (1,) * (len(shape) - axis_at - 1))

    level = one(*pieces[0])
    for cut in pieces[1:]:
        level = level * one(*cut)
    return level


def gaussian(rng, shape, deviation, most, pieces=(), held_as=jnp.bfloat16):
    values = deviation * jax.random.normal(rng, shape, jnp.float32)
    if pieces:
        values = values * shard_levels(rng, shape, pieces, -0.22, 0.18)
    return jnp.clip(values, -most, most).astype(held_as)


def gaussian_with(stream_key, shape, width, reach, pieces, heavy, kind=jnp.bfloat16):
    array = width * jax.random.normal(stream_key, shape, jnp.float32)
    if pieces:
        array = array * shard_levels(stream_key, shape, pieces, -0.22, 0.18)
    return jnp.clip(spiked(array, jax.random.fold_in(stream_key, 3), *heavy), -reach, reach).astype(kind)


def setup_inputs(seed: int = 0) -> dict:
    splits = jax.random.split(jax.random.key(seed), 4)
    amplitudes = gaussian(splits[0], (OCC_ROWS, EF_PAIRS), 1.0, 6.0, ((0, 4), (1, 8)))
    integrals = gaussian_with(splits[1], (EF_PAIRS, AB_PAIRS), (EF_PAIRS // 2) ** -0.5, 0.09375, ((0, 8), (1, 4)), (0, 1, 8, 2.0))
    active = draw_active(jax.random.fold_in(splits[3], 71), 0)
    return dict(amplitudes=amplitudes, integrals=integrals, active=active)


def reference(amplitudes, integrals, active):
    row_tiles = active.shape[0]
    pair_tiles = active.shape[1]
    blocks = amplitudes.reshape(row_tiles, TILE, pair_tiles, TILE)
    weights = active.astype(amplitudes.dtype)[:, None, :, None]
    masked = (blocks * weights).reshape(row_tiles, TILE, pair_tiles * TILE)

    def one_tile(rows):
        return jnp.dot(rows, integrals, preferred_element_type=jnp.float32).astype(jnp.bfloat16)

    result = lax.map(one_tile, masked)
    return result.reshape(row_tiles * TILE, integrals.shape[1])
```

```python
import functools
import math

import jax
import jax.numpy as jnp
from jax import lax
from jax.experimental import pallas as pl
from jax.experimental.pallas import tpu as pltpu
from jax.sharding import PartitionSpec as P

TILE = 128
CHUNKS = 4
MESH = pl.DeviceIdType.MESH


def fast_side(count):
    side = math.isqrt(count)
    while count % side:
        side -= 1
    return side


def kernel(
    p, q, nz, active, a_hbm, b_hbm, out, a, raw, b, part, got, zsend, zrecv,
    a_sem, b_sem, own_sem, fwd_sem, recv_sem, give_sem, got_sem, zsend_sem, zrecv_sem, reach_sem,
):
    o = lax.axis_index("occ")
    v = lax.axis_index("vir")
    core, z = lax.rem(v, 2), lax.div(v, 2)
    pi, qi = lax.div(o, q), lax.rem(o, q)
    rows, depth = a.shape
    width = raw.shape[1]
    sub = width // CHUNKS
    deep = depth // CHUNKS
    tall = rows // CHUNKS
    short = tall // 2
    per_core = CHUNKS // 2
    halves = (pl.ds(0, deep // 2), pl.ds(deep // 2, deep // 2))
    sibling = (o, v + 1 - 2 * core)
    below, above = (o, v - 2), (o, v + 2)
    f32 = jnp.float32

    def occ_at(dp, dq):
        return lax.rem(pi + dp, p) * q + lax.rem(qi + dq, q)

    def slot(dp, dq):
        return (dp % p) * q + dq % q

    def signal(sem, peer):
        pl.semaphore_signal(sem, inc=1, device_id=peer, device_id_type=MESH)

    b_copy = pltpu.make_async_copy(b_hbm, raw, b_sem)
    b_copy.start()
    a_copy = pltpu.make_async_copy(a_hbm, a, a_sem)
    a_copy.start()

    barrier = pltpu.get_barrier_semaphore()
    near = [sibling]
    near += [(occ_at(0, d), v) for d in range(1, q)]
    near += [(occ_at(d, 0), v) for d in range(1, p)]
    for peer in near:
        signal(barrier, peer)
    pl.when(z > 0)(lambda: signal(barrier, below))
    pl.when(z < nz - 1)(lambda: signal(barrier, above))

    def group_of(shape):
        return lax.div(lax.broadcasted_iota(jnp.int32, shape, 1), sub)

    b_copy.wait()
    group = group_of((deep, width))
    quarters = [raw[k * deep : (k + 1) * deep].astype(f32) for k in range(CHUNKS)]
    for j in range(CHUNKS):
        packed = None
        for k in range(CHUNKS):
            turn = (sub * (k - j)) % width
            piece = pltpu.roll(quarters[k], turn, 1) if turn else quarters[k]
            packed = piece if packed is None else jnp.where(group == k, piece, packed)
        b[0, j] = packed.astype(b.dtype)

    beside = lax.div(z + nz - 1, nz) + lax.div(2 * nz - 2 - z, nz)
    pl.semaphore_wait(barrier, len(near) + beside)

    sends = []

    def remote(src, dst, send_sem, to_sem, peer):
        copy = pltpu.make_async_remote_copy(
            src_ref=src, dst_ref=dst, send_sem=send_sem, recv_sem=to_sem,
            device_id=peer, device_id_type=MESH,
        )
        copy.start()
        return copy

    def send_own(j, stage):
        if j >= CHUNKS:
            return
        moves = [(0, d, stage) for d in range(1, q)] + [(d, 0, 1 - stage) for d in range(1, p)]
        for dp, dq, h in moves:
            s = slot(-dp, -dq)
            sends.append(
                remote(
                    b.at[0, j, halves[h]], b.at[s, j, halves[h]],
                    own_sem.at[s, j, h], recv_sem.at[s, j, h], (occ_at(dp, dq), v),
                )
            )

    def forward(sp, sq, dp, dq, j, h):
        s, t = slot(sp, sq), slot(sp - dp, sq - dq)
        sends.append(
            remote(
                b.at[s, j, halves[h]], b.at[t, j, halves[h]],
                fwd_sem.at[t, j, h], recv_sem.at[t, j, h], (occ_at(dp, dq), v),
            )
        )

    def arrived(dp, dq, j, h):
        s = slot(dp, dq)
        place = b.at[s, j, halves[h]]
        pltpu.make_async_copy(place, place, recv_sem.at[s, j, h]).wait()

    def reach(step):
        pl.when(z > 0)(lambda: signal(reach_sem.at[step, 1], below))
        pl.when(z < nz - 1)(lambda: signal(reach_sem.at[step, 0], above))

    def reached(step):
        pl.when(z > 0)(lambda: pl.semaphore_wait(reach_sem.at[step, 0], 1))
        pl.when(z < nz - 1)(lambda: pl.semaphore_wait(reach_sem.at[step, 1], 1))

    send_own(0, 0)
    send_own(0, 1)
    send_own(1, 0)
    reach(0)

    a_copy.wait()
    for r in range(rows // TILE):
        for e in range(depth // TILE):
            place = (pl.ds(r * TILE, TILE), pl.ds(e * TILE, TILE))
            weight = active[r, e].astype(f32)
            a[place] = (a[place].astype(f32) * weight).astype(a.dtype)

    for step in range(1, nz - 1):
        reached(step - 1)
        reach(step)
    lanes = group_of((tall, width))

    def multiply(dp, dq, j):
        s = slot(dp, dq)
        block = b[s, j]
        parts = [
            jnp.dot(a[:, k * deep : (k + 1) * deep], block, preferred_element_type=f32)
            for k in range(CHUNKS)
        ]
        summed = None
        for d in range(CHUNKS):
            mixed = None
            for k in range(CHUNKS):
                r = (k + d) % CHUNKS
                piece = parts[k][r * tall : (r + 1) * tall]
                mixed = piece if mixed is None else jnp.where(lanes == k, piece, mixed)
            mixed = pltpu.roll(mixed, sub * d, 1) if d else mixed
            summed = mixed if summed is None else summed + mixed
        part[s, j, 0] = summed[:short]
        part[s, j, 1] = summed[short:]
        copy = remote(
            part.at[s, j, 1 - core], got.at[s, j], give_sem.at[s, j], got_sem.at[s, j], sibling
        )
        return dp, dq, j, copy

    def z_copy(dp, dq, j):
        s = slot(dp, dq)
        owner = occ_at(dp, dq)
        place = lax.rem(z - owner + nz, nz)
        keeper = j // per_core
        return pltpu.make_async_remote_copy(
            src_ref=zsend.at[s, j],
            dst_ref=zrecv.at[j % per_core, place, core],
            send_sem=zsend_sem.at[s, j],
            recv_sem=zrecv_sem.at[j % per_core, place, core],
            device_id=(o, owner * 2 + keeper),
            device_id_type=MESH,
        )

    def stays(dp, dq, j):
        return occ_at(dp, dq) * 2 + j // per_core == v

    def hand_over(dp, dq, j, copy):
        s = slot(dp, dq)
        copy.wait()
        value = part[s, j, core] + got[s, j]

        @pl.when(stays(dp, dq, j))
        def _():
            zrecv[j % per_core, 0, core] = value

        @pl.when(jnp.logical_not(stays(dp, dq, j)))
        def _():
            zsend[s, j] = value
            z_copy(dp, dq, j).start()

    pending = []

    def run(dp, dq, j):
        pending.append(multiply(dp, dq, j))
        while len(pending) > 1:
            hand_over(*pending.pop(0))

    def diagonals(j):
        for dp in range(1, p):
            for dq in range(1, q):
                arrived(dp, dq, j, 0)
                arrived(dp, dq, j, 1)
                run(dp, dq, j)

    first = multiply(0, 0, 0)
    pending.append(first)
    reached(nz - 2)
    for j in range(CHUNKS):
        for d in range(1, q):
            arrived(0, d, j, 0)
            for f in range(1, p):
                forward(0, d, f, 0, j, 0)
        for d in range(1, p):
            arrived(d, 0, j, 1)
            for f in range(1, q):
                forward(d, 0, 0, f, j, 1)
        send_own(j + 1, 1)
        send_own(j + 2, 0)
        if j:
            diagonals(j - 1)
        if j + 1 < CHUNKS:
            run(0, 0, j + 1)
        for d in range(1, q):
            arrived(0, d, j, 1)
            run(0, d, j)
        for d in range(1, p):
            arrived(d, 0, j, 0)
            run(d, 0, j)
    while pending:
        hand_over(*pending.pop(0))
    diagonals(CHUNKS - 1)
    while pending:
        hand_over(*pending.pop(0))

    sums = {}
    for g in range(per_core):
        for k in range(2):
            for d in range(nz):

                def wait(g=g, d=d, k=k):
                    place = zrecv.at[g, d, k]
                    pltpu.make_async_copy(place, place, zrecv_sem.at[g, d, k]).wait()

                if d:
                    wait()
                else:
                    pl.when(core != k)(wait)
            total = zrecv[g, 0, k]
            for d in range(1, nz):
                total = total + zrecv[g, d, k]
            sums[g, k] = total
    small = group_of((short, width))
    for r in range(CHUNKS):
        for k in range(2):
            value = None
            for g in range(per_core):
                turn = (sub * (g - r)) % width
                piece = pltpu.roll(sums[g, k], turn, 1) if turn else sums[g, k]
                value = piece if value is None else jnp.where(small == g, piece, value)
            start = r * tall + k * short
            out[:, start : start + short] = value.T[: width // 2].astype(out.dtype)

    for copy in sends:
        copy.wait_send()
    for j in range(CHUNKS):
        for dp in range(p):
            for dq in range(q):

                @pl.when(jnp.logical_not(stays(dp, dq, j)))
                def _():
                    z_copy(dp, dq, j).wait_send()


def on_device(nocc, nvir, amplitudes, integrals, active):
    rows, depth = amplitudes.shape
    width = integrals.shape[1]
    q = fast_side(nocc)
    p = nocc // q
    nz = nvir // 2
    g = CHUNKS
    short = rows // g // 2
    f32 = jnp.float32
    any_space = pl.BlockSpec(memory_space=pl.ANY)
    dma = pltpu.SemaphoreType.DMA
    result = pl.pallas_call(
        functools.partial(kernel, p, q, nz),
        out_shape=pltpu.VMEM((width // 2, rows), jnp.bfloat16),
        in_specs=[pl.BlockSpec(memory_space=pltpu.SMEM), any_space, any_space],
        out_specs=pl.BlockSpec(memory_space=pltpu.VMEM),
        scratch_shapes=[
            pltpu.VMEM((rows, depth), amplitudes.dtype),
            pltpu.VMEM((depth, width), integrals.dtype),
            pltpu.VMEM((nocc, g, depth // g, width), integrals.dtype),
            pltpu.VMEM((nocc, g, 2, short, width), f32),
            pltpu.VMEM((nocc, g, short, width), f32),
            pltpu.VMEM((nocc, g, short, width), f32),
            pltpu.VMEM((g // 2, nz, 2, short, width), f32),
            dma(()), dma(()),
            dma((nocc, g, 2)), dma((nocc, g, 2)), dma((nocc, g, 2)),
            dma((nocc, g)), dma((nocc, g)), dma((nocc, g)), dma((g // 2, nz, 2)),
            pltpu.SemaphoreType.REGULAR((nz - 1, 2)),
        ],
        compiler_params=pltpu.CompilerParams(
            collective_id=0, has_side_effects=True
        ),
    )(active, amplitudes, integrals)
    return result.T


def solution(mesh):
    nocc, nvir = mesh.shape["occ"], mesh.shape["vir"]
    return jax.shard_map(
        functools.partial(on_device, nocc, nvir),
        mesh=mesh,
        in_specs=(P("occ", "vir"), P("vir", "occ"), P("occ", "vir")),
        out_specs=P("occ", "vir"),
        check_vma=False,
    )
```

```python
import functools
import math

import jax
import jax.numpy as jnp
from jax import lax
from jax.experimental import pallas as pl
from jax.experimental.pallas import tpu as pltpu
from jax.sharding import PartitionSpec as P

TILE = 128
CHUNKS = 4
MESH = pl.DeviceIdType.MESH


def fast_side(count):
    side = math.isqrt(count)
    while count % side:
        side -= 1
    return side


def kernel(
    p, q, nz, active_hbm, a_hbm, b_hbm, out, active, active_sem, a, raw, b, part, got, zsend, zrecv,
    a_sem, b_sem, own_sem, fwd_sem, recv_sem, give_sem, got_sem, zsend_sem, zrecv_sem, reach_sem,
):
    o = lax.axis_index("occ")
    v = lax.axis_index("vir")
    core, z = lax.rem(v, 2), lax.div(v, 2)
    pi, qi = lax.div(o, q), lax.rem(o, q)
    rows, depth = a.shape
    width = raw.shape[1]
    sub = width // CHUNKS
    deep = depth // CHUNKS
    tall = rows // CHUNKS
    short = tall // 2
    per_core = CHUNKS // 2
    halves = (pl.ds(0, deep // 2), pl.ds(deep // 2, deep // 2))
    sibling = (o, v + 1 - 2 * core)
    below, above = (o, v - 2), (o, v + 2)
    f32 = jnp.float32

    def occ_at(dp, dq):
        return lax.rem(pi + dp, p) * q + lax.rem(qi + dq, q)

    def slot(dp, dq):
        return (dp % p) * q + dq % q

    def signal(sem, peer):
        pl.semaphore_signal(sem, inc=1, device_id=peer, device_id_type=MESH)

    b_copy = pltpu.make_async_copy(b_hbm, raw, b_sem)
    b_copy.start()

    barrier = pltpu.get_barrier_semaphore()
    near = [sibling]
    near += [(occ_at(0, d), v) for d in range(1, q)]
    near += [(occ_at(d, 0), v) for d in range(1, p)]
    for peer in near:
        signal(barrier, peer)
    pl.when(z > 0)(lambda: signal(barrier, below))
    pl.when(z < nz - 1)(lambda: signal(barrier, above))

    a_copy = pltpu.make_async_copy(a_hbm, a, a_sem)
    a_copy.start()
    active_copy = pltpu.make_async_copy(active_hbm, active, active_sem)
    active_copy.start()

    def group_of(shape):
        return lax.div(lax.broadcasted_iota(jnp.int32, shape, 1), sub)

    b_copy.wait()
    group = group_of((deep, width))
    quarters = [raw[k * deep : (k + 1) * deep].astype(f32) for k in range(CHUNKS)]

    def pack(j):
        packed = None
        for k in range(CHUNKS):
            turn = (sub * (k - j)) % width
            piece = pltpu.roll(quarters[k], turn, 1) if turn else quarters[k]
            packed = piece if packed is None else jnp.where(group == k, piece, packed)
        b[0, j] = packed.astype(b.dtype)

    pack(0)
    beside = lax.div(z + nz - 1, nz) + lax.div(2 * nz - 2 - z, nz)
    pl.semaphore_wait(barrier, len(near) + beside)

    sends = []

    def remote(src, dst, send_sem, to_sem, peer):
        copy = pltpu.make_async_remote_copy(
            src_ref=src, dst_ref=dst, send_sem=send_sem, recv_sem=to_sem,
            device_id=peer, device_id_type=MESH,
        )
        copy.start()
        return copy

    def send_own(j, stage):
        if j >= CHUNKS:
            return
        moves = [(0, d, stage) for d in range(1, q)] + [(d, 0, 1 - stage) for d in range(1, p)]
        for dp, dq, h in moves:
            s = slot(-dp, -dq)
            sends.append(
                remote(
                    b.at[0, j, halves[h]], b.at[s, j, halves[h]],
                    own_sem.at[s, j, h], recv_sem.at[s, j, h], (occ_at(dp, dq), v),
                )
            )

    def forward(sp, sq, dp, dq, j, h):
        s, t = slot(sp, sq), slot(sp - dp, sq - dq)
        sends.append(
            remote(
                b.at[s, j, halves[h]], b.at[t, j, halves[h]],
                fwd_sem.at[t, j, h], recv_sem.at[t, j, h], (occ_at(dp, dq), v),
            )
        )

    def arrived(dp, dq, j, h):
        s = slot(dp, dq)
        place = b.at[s, j, halves[h]]
        pltpu.make_async_copy(place, place, recv_sem.at[s, j, h]).wait()

    def reach(step):
        pl.when(z > 0)(lambda: signal(reach_sem.at[step, 1], below))
        pl.when(z < nz - 1)(lambda: signal(reach_sem.at[step, 0], above))

    def reached(step):
        pl.when(z > 0)(lambda: pl.semaphore_wait(reach_sem.at[step, 0], 1))
        pl.when(z < nz - 1)(lambda: pl.semaphore_wait(reach_sem.at[step, 1], 1))

    send_own(0, 0)
    send_own(0, 1)
    reach(0)
    pack(1)
    send_own(1, 0)
    for j in range(2, CHUNKS):
        pack(j)

    a_copy.wait()
    active_copy.wait()
    for r in range(rows // TILE):
        for e in range(depth // TILE):
            place = (pl.ds(r * TILE, TILE), pl.ds(e * TILE, TILE))
            weight = active[r, e].astype(f32)
            a[place] = a[place] * jnp.full((TILE, TILE), weight, f32).astype(a.dtype)

    for step in range(1, nz - 1):
        reached(step - 1)
        reach(step)
    lanes = group_of((tall, width))

    def multiply(dp, dq, j):
        s = slot(dp, dq)
        block = b[s, j]
        parts = [
            jnp.dot(a[:, k * deep : (k + 1) * deep], block, preferred_element_type=f32)
            for k in range(CHUNKS)
        ]
        summed = None
        for d in range(CHUNKS):
            mixed = None
            for k in range(CHUNKS):
                r = (k + d) % CHUNKS
                piece = parts[k][r * tall : (r + 1) * tall]
                mixed = piece if mixed is None else jnp.where(lanes == k, piece, mixed)
            mixed = pltpu.roll(mixed, sub * d, 1) if d else mixed
            summed = mixed if summed is None else summed + mixed
        part[s, j, 0] = summed[:short]
        part[s, j, 1] = summed[short:]
        copy = remote(
            part.at[s, j, 1 - core], got.at[s, j], give_sem.at[s, j], got_sem.at[s, j], sibling
        )
        return dp, dq, j, copy

    def z_copy(dp, dq, j):
        s = slot(dp, dq)
        owner = occ_at(dp, dq)
        place = lax.rem(z - owner + nz, nz)
        keeper = j // per_core
        return pltpu.make_async_remote_copy(
            src_ref=zsend.at[s, j],
            dst_ref=zrecv.at[j % per_core, place, core],
            send_sem=zsend_sem.at[s, j],
            recv_sem=zrecv_sem.at[j % per_core, place, core],
            device_id=(o, owner * 2 + keeper),
            device_id_type=MESH,
        )

    def stays(dp, dq, j):
        return occ_at(dp, dq) * 2 + j // per_core == v

    def hand_over(dp, dq, j, copy):
        s = slot(dp, dq)
        copy.wait()
        value = part[s, j, core] + got[s, j]

        @pl.when(stays(dp, dq, j))
        def _():
            zrecv[j % per_core, 0, core] = value

        @pl.when(jnp.logical_not(stays(dp, dq, j)))
        def _():
            zsend[s, j] = value
            z_copy(dp, dq, j).start()

    pending = []

    def run(dp, dq, j):
        pending.append(multiply(dp, dq, j))
        while len(pending) > 1:
            hand_over(*pending.pop(0))

    def diagonals(j):
        for dp in range(1, p):
            for dq in range(1, q):
                arrived(dp, dq, j, 0)
                arrived(dp, dq, j, 1)
                run(dp, dq, j)

    first = multiply(0, 0, 0)
    pending.append(first)
    reached(nz - 2)
    for j in range(CHUNKS):
        for d in range(1, q):
            arrived(0, d, j, 0)
            for f in range(1, p):
                forward(0, d, f, 0, j, 0)
        for d in range(1, p):
            arrived(d, 0, j, 1)
            for f in range(1, q):
                forward(d, 0, 0, f, j, 1)
        send_own(j + 1, 1)
        send_own(j + 2, 0)
        if j:
            diagonals(j - 1)
        if j + 1 < CHUNKS:
            run(0, 0, j + 1)
        for d in range(1, q):
            arrived(0, d, j, 1)
            run(0, d, j)
        for d in range(1, p):
            arrived(d, 0, j, 0)
            run(d, 0, j)
    while pending:
        hand_over(*pending.pop(0))
    diagonals(CHUNKS - 1)
    while pending:
        hand_over(*pending.pop(0))

    sums = {}
    for g in range(per_core):
        for k in range(2):
            for d in range(nz):

                def wait(g=g, d=d, k=k):
                    place = zrecv.at[g, d, k]
                    pltpu.make_async_copy(place, place, zrecv_sem.at[g, d, k]).wait()

                if d:
                    wait()
                else:
                    pl.when(core != k)(wait)
            total = zrecv[g, 0, k]
            for d in range(1, nz):
                total = total + zrecv[g, d, k]
            sums[g, k] = total
    small = group_of((short, width))
    for r in range(CHUNKS):
        for k in range(2):
            value = None
            for g in range(per_core):
                turn = (sub * (g - r)) % width
                piece = pltpu.roll(sums[g, k], turn, 1) if turn else sums[g, k]
                value = piece if value is None else jnp.where(small == g, piece, value)
            start = r * tall + k * short
            out[:, start : start + short] = value.T[: width // 2].astype(out.dtype)

    for copy in sends:
        copy.wait_send()
    for j in range(CHUNKS):
        for dp in range(p):
            for dq in range(q):

                @pl.when(jnp.logical_not(stays(dp, dq, j)))
                def _():
                    z_copy(dp, dq, j).wait_send()


def on_device(nocc, nvir, amplitudes, integrals, active):
    rows, depth = amplitudes.shape
    width = integrals.shape[1]
    q = fast_side(nocc)
    p = nocc // q
    nz = nvir // 2
    g = CHUNKS
    short = rows // g // 2
    f32 = jnp.float32
    any_space = pl.BlockSpec(memory_space=pl.ANY)
    dma = pltpu.SemaphoreType.DMA
    result = pl.pallas_call(
        functools.partial(kernel, p, q, nz),
        out_shape=pltpu.VMEM((width // 2, rows), jnp.bfloat16),
        in_specs=[any_space, any_space, any_space],
        out_specs=pl.BlockSpec(memory_space=pltpu.VMEM),
        scratch_shapes=[
            pltpu.SMEM(active.shape, active.dtype), dma(()),
            pltpu.VMEM((rows, depth), amplitudes.dtype),
            pltpu.VMEM((depth, width), integrals.dtype),
            pltpu.VMEM((nocc, g, depth // g, width), integrals.dtype),
            pltpu.VMEM((nocc, g, 2, short, width), f32),
            pltpu.VMEM((nocc, g, short, width), f32),
            pltpu.VMEM((nocc, g, short, width), f32),
            pltpu.VMEM((g // 2, nz, 2, short, width), f32),
            dma(()), dma(()),
            dma((nocc, g, 2)), dma((nocc, g, 2)), dma((nocc, g, 2)),
            dma((nocc, g)), dma((nocc, g)), dma((nocc, g)), dma((g // 2, nz, 2)),
            pltpu.SemaphoreType.REGULAR((nz - 1, 2)),
        ],
        compiler_params=pltpu.CompilerParams(
            collective_id=0, has_side_effects=True
        ),
    )(active, amplitudes, integrals)
    return result.T


def solution(mesh):
    nocc, nvir = mesh.shape["occ"], mesh.shape["vir"]
    return jax.shard_map(
        functools.partial(on_device, nocc, nvir),
        mesh=mesh,
        in_specs=(P("occ", "vir"), P("vir", "occ"), P("occ", "vir")),
        out_specs=P("occ", "vir"),
        check_vma=False,
    )
```

```python
import functools
import math

import jax
import jax.numpy as jnp
from jax import lax
from jax.experimental import pallas as pl
from jax.experimental.pallas import tpu as pltpu
from jax.sharding import PartitionSpec as P

TILE = 128
CHUNKS = 4
MESH = pl.DeviceIdType.MESH


def fast_side(count):
    side = math.isqrt(count)
    while count % side:
        side -= 1
    return side


def kernel(
    p, q, nz, active_hbm, a_hbm, b_hbm, out, active, active_sem, a, raw, b, part, got, zsend, zrecv,
    a_sem, b_sem, own_sem, fwd_sem, recv_sem, give_sem, got_sem, zsend_sem, zrecv_sem, reach_sem,
):
    o = lax.axis_index("occ")
    v = lax.axis_index("vir")
    core, z = lax.rem(v, 2), lax.div(v, 2)
    pi, qi = lax.div(o, q), lax.rem(o, q)
    rows, depth = a.shape
    width = raw.shape[1]
    sub = width // CHUNKS
    deep = depth // CHUNKS
    tall = rows // CHUNKS
    short = tall // 2
    per_core = CHUNKS // 2
    halves = (pl.ds(0, deep // 2), pl.ds(deep // 2, deep // 2))
    sibling = (o, v + 1 - 2 * core)
    below, above = (o, v - 2), (o, v + 2)
    f32 = jnp.float32

    def occ_at(dp, dq):
        return lax.rem(pi + dp, p) * q + lax.rem(qi + dq, q)

    def slot(dp, dq):
        return (dp % p) * q + dq % q

    def signal(sem, peer):
        pl.semaphore_signal(sem, inc=1, device_id=peer, device_id_type=MESH)

    b_copy = pltpu.make_async_copy(b_hbm, raw, b_sem)
    b_copy.start()

    barrier = pltpu.get_barrier_semaphore()
    near = [sibling]
    near += [(occ_at(0, d), v) for d in range(1, q)]
    near += [(occ_at(d, 0), v) for d in range(1, p)]
    for peer in near:
        signal(barrier, peer)
    pl.when(z > 0)(lambda: signal(barrier, below))
    pl.when(z < nz - 1)(lambda: signal(barrier, above))

    a_copy = pltpu.make_async_copy(a_hbm, a, a_sem)
    a_copy.start()
    active_copy = pltpu.make_async_copy(active_hbm, active, active_sem)
    active_copy.start()

    def group_of(shape):
        return lax.div(lax.broadcasted_iota(jnp.int32, shape, 1), sub)

    b_copy.wait()
    group = group_of((deep, width))
    quarters = [raw[k * deep : (k + 1) * deep].astype(f32) for k in range(CHUNKS)]

    def pack(j):
        packed = None
        for k in range(CHUNKS):
            turn = (sub * (k - j)) % width
            piece = pltpu.roll(quarters[k], turn, 1) if turn else quarters[k]
            packed = piece if packed is None else jnp.where(group == k, piece, packed)
        b[0, j] = packed.astype(b.dtype)

    pack(0)
    beside = lax.div(z + nz - 1, nz) + lax.div(2 * nz - 2 - z, nz)
    pl.semaphore_wait(barrier, len(near) + beside)

    sends = []

    def remote(src, dst, send_sem, to_sem, peer):
        copy = pltpu.make_async_remote_copy(
            src_ref=src, dst_ref=dst, send_sem=send_sem, recv_sem=to_sem,
            device_id=peer, device_id_type=MESH,
        )
        copy.start()
        return copy

    def send_own(j, stage):
        if j >= CHUNKS:
            return
        moves = [(0, d, stage) for d in range(1, q)] + [(d, 0, 1 - stage) for d in range(1, p)]
        for dp, dq, h in moves:
            s = slot(-dp, -dq)
            sends.append(
                remote(
                    b.at[0, j, halves[h]], b.at[s, j, halves[h]],
                    own_sem.at[s, j, h], recv_sem.at[s, j, h], (occ_at(dp, dq), v),
                )
            )

    def forward(sp, sq, dp, dq, j, h):
        s, t = slot(sp, sq), slot(sp - dp, sq - dq)
        sends.append(
            remote(
                b.at[s, j, halves[h]], b.at[t, j, halves[h]],
                fwd_sem.at[t, j, h], recv_sem.at[t, j, h], (occ_at(dp, dq), v),
            )
        )

    def arrived(dp, dq, j, h):
        s = slot(dp, dq)
        place = b.at[s, j, halves[h]]
        pltpu.make_async_copy(place, place, recv_sem.at[s, j, h]).wait()

    def reach(step):
        pl.when(z > 0)(lambda: signal(reach_sem.at[step, 1], below))
        pl.when(z < nz - 1)(lambda: signal(reach_sem.at[step, 0], above))

    def reached(step):
        pl.when(z > 0)(lambda: pl.semaphore_wait(reach_sem.at[step, 0], 1))
        pl.when(z < nz - 1)(lambda: pl.semaphore_wait(reach_sem.at[step, 1], 1))

    send_own(0, 0)
    send_own(0, 1)
    reach(0)
    pack(1)
    send_own(1, 0)
    for j in range(2, CHUNKS):
        pack(j)

    a_copy.wait()
    active_copy.wait()
    for r in range(rows // TILE):
        for e in range(depth // TILE):
            place = (pl.ds(r * TILE, TILE), pl.ds(e * TILE, TILE))
            weight = active[r, e].astype(f32)
            a[place] = a[place] * jnp.full((TILE, TILE), weight, f32).astype(a.dtype)

    for step in range(1, nz - 1):
        reached(step - 1)
        reach(step)
    lanes = group_of((tall, width))

    def multiply(dp, dq, j):
        s = slot(dp, dq)
        block = b[s, j]
        parts = [
            jnp.dot(a[:, k * deep : (k + 1) * deep], block, preferred_element_type=f32)
            for k in range(CHUNKS)
        ]
        summed = None
        for d in range(CHUNKS):
            mixed = None
            for k in range(CHUNKS):
                r = (k + d) % CHUNKS
                piece = parts[k][r * tall : (r + 1) * tall]
                mixed = piece if mixed is None else jnp.where(lanes == k, piece, mixed)
            mixed = pltpu.roll(mixed, sub * d, 1) if d else mixed
            summed = mixed if summed is None else summed + mixed
        part[s, j, 0] = summed[:short]
        part[s, j, 1] = summed[short:]
        copy = remote(
            part.at[s, j, 1 - core], got.at[s, j], give_sem.at[s, j], got_sem.at[s, j], sibling
        )
        return dp, dq, j, copy

    def z_copy(dp, dq, j):
        s = slot(dp, dq)
        owner = occ_at(dp, dq)
        place = lax.rem(z - owner + nz, nz)
        keeper = j // per_core
        return pltpu.make_async_remote_copy(
            src_ref=zsend.at[s, j],
            dst_ref=zrecv.at[j % per_core, place, core],
            send_sem=zsend_sem.at[s, j],
            recv_sem=zrecv_sem.at[j % per_core, place, core],
            device_id=(o, owner * 2 + keeper),
            device_id_type=MESH,
        )

    def stays(dp, dq, j):
        return occ_at(dp, dq) * 2 + j // per_core == v

    def hand_over(dp, dq, j, copy):
        s = slot(dp, dq)
        copy.wait()
        value = part[s, j, core] + got[s, j]

        @pl.when(stays(dp, dq, j))
        def _():
            zrecv[j % per_core, 0, core] = value

        @pl.when(jnp.logical_not(stays(dp, dq, j)))
        def _():
            zsend[s, j] = value
            z_copy(dp, dq, j).start()

    pending = []

    def run(dp, dq, j):
        pending.append(multiply(dp, dq, j))
        while len(pending) > 2:
            hand_over(*pending.pop(0))

    def diagonals(j):
        for dp in range(1, p):
            for dq in range(1, q):
                arrived(dp, dq, j, 0)
                arrived(dp, dq, j, 1)
                run(dp, dq, j)

    first = multiply(0, 0, 0)
    pending.append(first)
    reached(nz - 2)
    for j in range(CHUNKS):
        for d in range(1, q):
            arrived(0, d, j, 0)
            for f in range(1, p):
                forward(0, d, f, 0, j, 0)
        for d in range(1, p):
            arrived(d, 0, j, 1)
            for f in range(1, q):
                forward(d, 0, 0, f, j, 1)
        send_own(j + 1, 1)
        send_own(j + 2, 0)
        if j:
            diagonals(j - 1)
        if j + 1 < CHUNKS:
            run(0, 0, j + 1)
        for d in range(1, q):
            arrived(0, d, j, 1)
            run(0, d, j)
        for d in range(1, p):
            arrived(d, 0, j, 0)
            run(d, 0, j)
    while pending:
        hand_over(*pending.pop(0))
    diagonals(CHUNKS - 1)
    while pending:
        hand_over(*pending.pop(0))

    sums = {}
    for g in range(per_core):
        for k in range(2):
            for d in range(nz):

                def wait(g=g, d=d, k=k):
                    place = zrecv.at[g, d, k]
                    pltpu.make_async_copy(place, place, zrecv_sem.at[g, d, k]).wait()

                if d:
                    wait()
                else:
                    pl.when(core != k)(wait)
            total = zrecv[g, 0, k]
            for d in range(1, nz):
                total = total + zrecv[g, d, k]
            sums[g, k] = total
    small = group_of((short, width))
    for r in range(CHUNKS):
        for k in range(2):
            value = None
            for g in range(per_core):
                turn = (sub * (g - r)) % width
                piece = pltpu.roll(sums[g, k], turn, 1) if turn else sums[g, k]
                value = piece if value is None else jnp.where(small == g, piece, value)
            start = r * tall + k * short
            out[:, start : start + short] = value.T[: width // 2].astype(out.dtype)

    for copy in sends:
        copy.wait_send()
    for j in range(CHUNKS):
        for dp in range(p):
            for dq in range(q):

                @pl.when(jnp.logical_not(stays(dp, dq, j)))
                def _():
                    z_copy(dp, dq, j).wait_send()


def on_device(nocc, nvir, amplitudes, integrals, active):
    rows, depth = amplitudes.shape
    width = integrals.shape[1]
    q = fast_side(nocc)
    p = nocc // q
    nz = nvir // 2
    g = CHUNKS
    short = rows // g // 2
    f32 = jnp.float32
    any_space = pl.BlockSpec(memory_space=pl.ANY)
    dma = pltpu.SemaphoreType.DMA
    result = pl.pallas_call(
        functools.partial(kernel, p, q, nz),
        out_shape=pltpu.VMEM((width // 2, rows), jnp.bfloat16),
        in_specs=[any_space, any_space, any_space],
        out_specs=pl.BlockSpec(memory_space=pltpu.VMEM),
        scratch_shapes=[
            pltpu.SMEM(active.shape, active.dtype), dma(()),
            pltpu.VMEM((rows, depth), amplitudes.dtype),
            pltpu.VMEM((depth, width), integrals.dtype),
            pltpu.VMEM((nocc, g, depth // g, width), integrals.dtype),
            pltpu.VMEM((nocc, g, 2, short, width), f32),
            pltpu.VMEM((nocc, g, short, width), f32),
            pltpu.VMEM((nocc, g, short, width), f32),
            pltpu.VMEM((g // 2, nz, 2, short, width), f32),
            dma(()), dma(()),
            dma((nocc, g, 2)), dma((nocc, g, 2)), dma((nocc, g, 2)),
            dma((nocc, g)), dma((nocc, g)), dma((nocc, g)), dma((g // 2, nz, 2)),
            pltpu.SemaphoreType.REGULAR((nz - 1, 2)),
        ],
        compiler_params=pltpu.CompilerParams(
            collective_id=0, has_side_effects=True
        ),
    )(active, amplitudes, integrals)
    return result.T


def solution(mesh):
    nocc, nvir = mesh.shape["occ"], mesh.shape["vir"]
    return jax.shard_map(
        functools.partial(on_device, nocc, nvir),
        mesh=mesh,
        in_specs=(P("occ", "vir"), P("vir", "occ"), P("occ", "vir")),
        out_specs=P("occ", "vir"),
        check_vma=False,
    )
```
